256 devices in a mesh: row: 32 (over x, y, core), col: 8 (over z).
Axes of the slice: x: 4, y: 4, z: 8, core: 2. Of those that a mesh axis runs over, the one named last changes fastest.
Arguments:
- inputs: bfloat16 [16384, 1792], P(('row', 'col')), may hold values from -6 to 6
- attention_norm_gain: float32 [1792], replicated, may hold values from 0.5 to 1.5
- query_key_value_weight: bfloat16 [1792, 3, 1792], P('row', None, 'col'), may hold values from -0.125 to 0.125
- filter_taps: float32 [3, 2, 1792], P(None, None, 'col'), may hold values from -3 to 3
- output_projection: bfloat16 [1792, 1792], P('col', 'row'), may hold values from -0.125 to 0.125
- window_key_value: bfloat16 [256, 2, 16, 7168], P('row', None, 'col'), may hold values from -300 to 300
- cache_valid_length: int32 [256], P('row'), may hold values from 0 to 64
- lengths: int32 [32, 8], P('row'), may hold values from 1 to 128, 512 in all within a row
- token_adapter_index: int32 [16384, 1], P('row'), may hold values from 0 to 63; in each aligned block of 64 rows (0 to 63, 64 to 127, ...) at most 2 rows name the same one
- adapter_down_map: bfloat16 [64, 1792, 16], P('row'), may hold values from -0.125 to 0.125
- adapter_up_map: bfloat16 [64, 16, 1792], P('row'), may hold values from -1.5 to 1.5
- feed_forward_gain: float32 [1792], replicated, may hold values from 0.5 to 1.5
- gate_projection: bfloat16 [1792, 4096], P('row', 'col'), may hold values from -0.125 to 0.125
- up_projection: bfloat16 [1792, 4096], P('row', 'col'), may hold values from -0.125 to 0.125
- down_projection: bfloat16 [4096, 1792], P('col', 'row'), may hold values from -0.09375 to 0.09375
Outputs:
- layer_out: bfloat16 [16384, 1792], P(('row', 'col'))
The draws below stay inside these ranges and needn't reach their ends.
Inputs may be any that keep to these rules, and one draw needn't show every extreme that they name: Each row of lengths sums to 512, and its largest entry is exactly 128. `cache_valid_length`: A request with 0 is a new prompt without cached positions. `token_adapter_index`: in each aligned block of 64 tokens no adapter serves more than 2 tokens, and some adapter serves exactly 2.
All inputs are finite; a program needn't handle non-finite values.
Results may differ from the reference program's by a relative error of at most 0.019.
Values may be sent and summed in bfloat16 or wider, within the bound.
A program may use at most 64 MiB of HBM per device.

```python
import math
import jax
import jax.numpy as jnp
import numpy as np
from jax import lax

MODEL_WIDTH = 1792
HEADS = 16
HD = 112
ATT = 1792
FF = 4096
WIN = 64
KSIZE = 3
ADAPTER_RANK = 16
ADAPTER_COUNT = 64
TOK_ROW = 512
TOKENS = 16384
REQ_ROW = 8
REQUESTS = 256
LEN_MOST = 128
BLOCK = 64
MOST = 2
N_ROW = 32
N_COL = 8


def draw_window_key_value(key, part):
    key_base = jax.random.fold_in(key, 11)
    whole = jnp.clip(jax.random.normal(key_base, (REQUESTS, 2, HEADS, WIN * HD), jnp.float32), -6.0, 6.0)
    return whole.astype(jnp.bfloat16)


def with_ends(entries, key, low, top_value):
    longest = entries.shape.index(max(entries.shape))
    spots = []
    for shift in (0, 1):
        where = [jax.random.randint(jax.random.fold_in(key, axis), (), 0, length) for axis, length in enumerate(entries.shape)]
        where[longest] = (where[longest] + shift) % entries.shape[longest]
        spots.append(tuple(where))
    return entries.at[spots[0]].set(low).at[spots[1]].set(top_value)


def steps_of(own_key, shape, split, smallest, largest):
    factor_of, own = 1.0, jax.random.fold_in(own_key, 6)
    for position, blocks in split:
        draws = jnp.exp(jax.random.uniform(jax.random.fold_in(own, position), (blocks,), jnp.float32, smallest / len(split), largest / len(split)))
        factor_of = factor_of * jnp.repeat(draws, shape[position] // blocks).reshape([-1 if axis == position else 1 for axis in range(len(shape))])
    return factor_of


def split_up(count, total, limit, skew):
    weights = [(1 << 20) // math.isqrt(standing ** skew) + 1 for standing in range(2, count + 1)]
    rest, counts = total - limit - (count - 1), [1] * (count - 1)
    while rest > 0:
        free = [i for i in range(count - 1) if counts[i] < limit]
        mass, remaining = sum([weights[i] for i in free]), rest
        for i in free:
            more = min(limit - counts[i], max(1, remaining * weights[i] // mass), rest)
            counts[i] = counts[i] + more
            rest = rest - more
    return np.array([limit] + counts)


def ragged_sizes(stream_key, number_of, total, limit, slope):
    if number_of == 2:
        one = jax.random.randint(stream_key, (), max(1, total - limit), min(limit, total - 1) + 1)
        return jnp.stack([one, total - one])
    sizes = jnp.asarray(split_up(number_of, total, limit, slope), jnp.int32)
    couples = (number_of - 1) // 2
    donor, receiver = sizes[1:1 + 2 * couples:2], sizes[2:2 + 2 * couples:2]
    slack = jnp.minimum(donor - 1, limit - receiver)
    passed = jax.random.randint(jax.random.fold_in(stream_key, 1), (couples,), 0, 1 << 20) % (slack + 1)
    sizes = sizes.at[1:1 + 2 * couples:2].set(donor - passed).at[2:2 + 2 * couples:2].set(receiver + passed)
    return sizes[jax.random.permutation(jax.random.fold_in(stream_key, 2), number_of)]


def shared_out(rng, own, number, rows, amount, top, bound, skew):
    sequence = jax.random.permutation(rng, amount)
    packed, common = shares(amount, rows * top, bound, skew, True), shares(amount, rows * top, bound, skew, False)
    places = jnp.arange(amount)

    def named(sizes, offset_by):
        used = int((sizes > 0).sum())
        fixed = max(1, used // 4)
        passed = fixed + (places - fixed + offset_by * (used - fixed)) % max(1, amount - fixed)
        return jnp.zeros((amount,), jnp.int32).at[sequence[jnp.where(places < fixed, places, passed)]].set(jnp.asarray(sizes, jnp.int32))

    sizes = jnp.where(number % 4 == 0, named(packed, number // 4), named(common, number - number // 4 - 1))
    mixed = jax.random.permutation(jax.random.fold_in(own, 3), amount)
    giver, receiver = mixed[0:amount // 2 * 2:2], mixed[1:amount // 2 * 2:2]
    slack = jnp.minimum(sizes[giver] - 1, bound - sizes[receiver]) // 2
    slack = jnp.where((giver == sequence[0]) | (receiver == sequence[0]) | (sizes[receiver] == 0), 0, jnp.maximum(slack, 0))
    passed = jax.random.randint(jax.random.fold_in(own, 4), (amount // 2,), 0, 1 << 20) % (slack + 1)
    sizes = sizes.at[giver].add(-passed).at[receiver].add(passed)
    items = jnp.searchsorted(jnp.cumsum(sizes), jnp.arange(rows * top), side="right").astype(jnp.int32)
    listing = items.reshape(top, rows).T
    listing = listing[jax.random.permutation(jax.random.fold_in(own, 1), rows)]
    offset_by = jax.random.randint(jax.random.fold_in(own, 2), (rows, 1), 0, top)
    return jnp.take_along_axis(listing, (jnp.arange(top)[None, :] + offset_by) % top, axis=1)


def shares(amount, total, reach, slope, full):
    weights = [(1 << 20) // math.isqrt(grade ** slope) + 1 for grade in range(1, amount + 1)]
    largest = reach if full else min(reach, max(-(-total // amount), total * weights[0] // sum(weights)))
    least = 1 if total - largest >= amount - 1 else 0
    given, surplus = [largest] + [least] * (amount - 1), total - largest - least * (amount - 1)
    while surplus > 0:
        candidates = [i for i in range(1, amount) if given[i] < largest] or [i for i in range(1, amount) if given[i] < reach]
        pool, left = sum([weights[i] for i in candidates]), surplus
        for i in candidates:
            extra = min(reach - given[i], max(1, left * weights[i] // pool), surplus)
            given[i] = given[i] + extra
            surplus = surplus - extra
    return np.array(given)


def bell_draw(key, extent, scale, reach, pieces=(), held_as=jnp.bfloat16):
    drawn = jax.random.normal(key, extent, jnp.float32) * scale
    if len(pieces) > 0:
        drawn = steps_of(key, extent, pieces, -0.22, 0.18) * drawn
    return jnp.clip(drawn, min=-reach, max=reach).astype(held_as)


def setup_inputs(seed: int = 0) -> dict:
    key_of = jax.random.split(jax.random.key(seed), 16)
    inputs = bell_draw(key_of[0], (TOKENS, MODEL_WIDTH), 1.0, 6.0, ((0, 256),))
    attention_norm_gain = jnp.clip(1.0 + 0.1 * jax.random.normal(key_of[1], (MODEL_WIDTH,), jnp.float32), 0.5, 1.5)
    query_key_value_weight = bell_draw(key_of[2], (MODEL_WIDTH, 3, ATT), MODEL_WIDTH ** -0.5, 0.125, ((0, 32), (2, 8)))
    filter_taps = bell_draw(key_of[3], (KSIZE, 2, ATT), 0.6, 3.0, ((2, 8),), jnp.float32)
    output_projection = bell_draw(key_of[4], (ATT, MODEL_WIDTH), ATT ** -0.5, 0.125, ((0, 8), (1, 32)))
    window_key_value = draw_window_key_value(jax.random.fold_in(key_of[15], 71), 0)
    cache_valid_length = with_ends(jax.random.randint(key_of[6], (REQUESTS,), 0, WIN + 1), jax.random.fold_in(key_of[6], 1), 0, WIN).astype(jnp.int32)
    lengths = jax.vmap(lambda own: ragged_sizes(own, REQ_ROW, TOK_ROW, LEN_MOST, 2))(jax.random.split(key_of[7], N_ROW)).reshape((N_ROW, REQ_ROW)).astype(jnp.int32)
    token_adapter_index_keys = jax.random.split(jax.random.fold_in(key_of[8], 1), TOKENS // BLOCK)
    token_adapter_index_turns = jax.random.permutation(jax.random.fold_in(key_of[8], 3), TOKENS // BLOCK)
    token_adapter_index = jax.vmap(lambda own, number: shared_out(jax.random.fold_in(key_of[8], 2), own, number, BLOCK, ADAPTER_COUNT, 1, MOST, 2))(token_adapter_index_keys, token_adapter_index_turns).reshape((TOKENS, 1))
    adapter_down_map = bell_draw(key_of[9], (ADAPTER_COUNT, MODEL_WIDTH, ADAPTER_RANK), MODEL_WIDTH ** -0.5, 0.125, ((0, 32),))
    adapter_up_map = bell_draw(key_of[10], (ADAPTER_COUNT, ADAPTER_RANK, MODEL_WIDTH), ADAPTER_RANK ** -0.5, 1.5, ((0, 32),))
    feed_forward_gain = jnp.clip(1.0 + 0.1 * jax.random.normal(key_of[11], (MODEL_WIDTH,), jnp.float32), 0.5, 1.5)
    gate_projection = bell_draw(key_of[12], (MODEL_WIDTH, FF), MODEL_WIDTH ** -0.5, 0.125, ((0, 32), (1, 8)))
    up_projection = bell_draw(key_of[13], (MODEL_WIDTH, FF), MODEL_WIDTH ** -0.5, 0.125, ((0, 32), (1, 8)))
    down_projection = bell_draw(key_of[14], (FF, MODEL_WIDTH), FF ** -0.5, 0.09375, ((0, 8), (1, 32)))
    return {"inputs": inputs, "attention_norm_gain": attention_norm_gain, "query_key_value_weight": query_key_value_weight, "filter_taps": filter_taps, "output_projection": output_projection, "window_key_value": window_key_value, "cache_valid_length": cache_valid_length, "lengths": lengths, "token_adapter_index": token_adapter_index, "adapter_down_map": adapter_down_map, "adapter_up_map": adapter_up_map, "feed_forward_gain": feed_forward_gain, "gate_projection": gate_projection, "up_projection": up_projection, "down_projection": down_projection}


epsilon = 1e-05

def rms_scaled(values, gain_row):
    mean_square = lax.optimization_barrier(jnp.mean(values * values, axis=-1, keepdims=True))
    return values * lax.rsqrt(mean_square + epsilon) * gain_row.astype(jnp.float32)

def layout(lengths_row, tok_count):
    finish = jnp.cumsum(lengths_row).astype(jnp.int32)
    begins = finish - lengths_row
    places = jnp.arange(tok_count, dtype=jnp.int32)
    segment = lax.optimization_barrier(jnp.sum((places[:, None] >= finish[None, :]).astype(jnp.int32), axis=1))
    member = segment[:, None] == jnp.arange(lengths_row.shape[0], dtype=jnp.int32)[None, :]
    inside = places - lax.optimization_barrier(jnp.sum(jnp.where(member, begins[None, :], 0), axis=1)).astype(jnp.int32)
    return (segment, inside)

def shifted(values, offset, inside):
    moved_rows = jnp.pad(values[:values.shape[0] - offset], ((offset, 0), (0, 0)))
    return jnp.where((inside >= offset)[:, None], moved_rows, jnp.zeros_like(moved_rows))

def convolve(values, taps, inside):
    running = jnp.zeros_like(values)
    for offset in range(taps.shape[0]):
        running = running + taps[offset][None, :] * shifted(values, offset, inside)
    return running

def make_qkv(qkv_mixed, filter_taps, inside):
    queries = qkv_mixed[:, 0].astype(jnp.bfloat16)
    keys_used = convolve(qkv_mixed[:, 1], filter_taps[:, 0], inside).astype(jnp.bfloat16)
    raw_values = qkv_mixed[:, 2]
    gates = jax.nn.sigmoid(convolve(raw_values, filter_taps[:, 1], inside))
    values_used = (raw_values * gates).astype(jnp.bfloat16)
    return (queries, keys_used, values_used)

def split_cache(window_key_value, head_size):
    requests_here, head_count = (window_key_value.shape[0], window_key_value.shape[2])
    window = window_key_value.shape[3] // head_size
    split_kv = window_key_value.reshape(requests_here, 2, head_count, window, head_size)
    cached_key_rows = jnp.transpose(split_kv[:, 0], (0, 2, 1, 3)).reshape(requests_here * window, head_count, head_size)
    cached_value_rows = jnp.transpose(split_kv[:, 1], (0, 2, 1, 3)).reshape(requests_here * window, head_count, head_size)
    return (cached_key_rows, cached_value_rows, window)

def attend(queries, keys_used, values_used, window_key_value, segment, inside, cache_valid_length, head_size):
    tok_count = queries.shape[0]
    head_count = queries.shape[1] // head_size
    requests_here = window_key_value.shape[0]
    cached_key_rows, cached_value_rows, window = split_cache(window_key_value, head_size)
    query_per_head = queries.reshape(tok_count, head_count, head_size).astype(jnp.float32)
    key_h = keys_used.reshape(tok_count, head_count, head_size).astype(jnp.float32)
    value_per_head = values_used.reshape(tok_count, head_count, head_size).astype(jnp.float32)
    cached_key_rows = cached_key_rows.astype(jnp.float32)
    cached_value_rows = cached_value_rows.astype(jnp.float32)
    attention_score_scale = head_size ** (-0.5)
    places = jnp.arange(tok_count, dtype=jnp.int32)
    local_mask = (segment[:, None] == segment[None, :]) & (places[None, :] <= places[:, None]) & (places[None, :] > places[:, None] - window)
    slot_ids = jnp.arange(requests_here * window, dtype=jnp.int32)
    owner_req = slot_ids // window
    within = slot_ids % window
    slot_ages = jnp.repeat(cache_valid_length, window)
    cache_mask = (segment[:, None] == owner_req[None, :]) & (within[None, :] >= window - slot_ages[None, :]) & (within[None, :] > inside[:, None])
    local_scores = jnp.einsum('thd,jhd->htj', query_per_head, key_h) * attention_score_scale
    cached_score_rows = jnp.einsum('sek,yek->esy', query_per_head, cached_key_rows) * attention_score_scale
    local_scores = jnp.where(local_mask[None], local_scores, -jnp.inf)
    cached_score_rows = jnp.where(cache_mask[None], cached_score_rows, -jnp.inf)
    row_max = jnp.maximum(lax.optimization_barrier(jnp.max(local_scores, axis=-1, keepdims=True)), lax.optimization_barrier(jnp.max(cached_score_rows, axis=-1, keepdims=True)))
    local_exp = jnp.exp(local_scores - row_max)
    cache_exp = jnp.exp(cached_score_rows - row_max)
    denominator = lax.optimization_barrier(jnp.sum(local_exp, axis=-1, keepdims=True)) + lax.optimization_barrier(jnp.sum(cache_exp, axis=-1, keepdims=True))
    window_attention_weight = (local_exp / denominator).astype(jnp.bfloat16).astype(jnp.float32)
    cached_attention_weight = (cache_exp / denominator).astype(jnp.bfloat16).astype(jnp.float32)
    joined_output = jnp.einsum('zkc,czu->kzu', window_attention_weight, value_per_head) + jnp.einsum('lar,rlx->alx', cached_attention_weight, cached_value_rows)
    return joined_output.reshape(tok_count, head_count * head_size).astype(jnp.bfloat16)

def apply_low_rank(normalized_input, adapter_row_picks, adapter_down_map, adapter_up_map):
    every_adapter = adapter_down_map.shape[0]
    member = (adapter_row_picks[:, None] == jnp.arange(every_adapter, dtype=jnp.int32)[None, :]).astype(jnp.float32)
    every_low_rank = jnp.einsum('lw,bwj->lbj', normalized_input.astype(jnp.float32), adapter_down_map.astype(jnp.float32))
    low = lax.optimization_barrier(jnp.sum(member[:, :, None] * every_low_rank, axis=1)).astype(jnp.bfloat16)
    widened_low_rank = member[:, :, None] * low.astype(jnp.float32)[:, None, :]
    return jnp.einsum('bhf,hfz->bz', widened_low_rank, adapter_up_map.astype(jnp.float32)).astype(jnp.bfloat16)

def reference(inputs, attention_norm_gain, query_key_value_weight, filter_taps, output_projection, window_key_value, cache_valid_length, lengths, token_adapter_index, adapter_down_map, adapter_up_map, feed_forward_gain, gate_projection, up_projection, down_projection):

    def one_group(row_group):
        token_rows = lax.dynamic_slice_in_dim(inputs, row_group * TOK_ROW, TOK_ROW, 0)
        normalized_input = rms_scaled(token_rows.astype(jnp.float32), attention_norm_gain).astype(jnp.bfloat16)
        qkv_mixed = jnp.einsum('td,dka->tka', normalized_input.astype(jnp.float32), query_key_value_weight.astype(jnp.float32))
        lengths_row = lax.dynamic_slice_in_dim(lengths, row_group, 1, 0)[0]
        segment, inside = layout(lengths_row, TOK_ROW)
        queries, keys_used, values_used = make_qkv(qkv_mixed, filter_taps, inside)
        cache_here = lax.dynamic_slice_in_dim(window_key_value, row_group * REQ_ROW, REQ_ROW, 0)
        ages_here = lax.dynamic_slice_in_dim(cache_valid_length, row_group * REQ_ROW, REQ_ROW, 0)
        attended = attend(queries, keys_used, values_used, cache_here, segment, inside, ages_here, HD)
        adapter_row_picks = lax.dynamic_slice_in_dim(token_adapter_index[:, 0], row_group * TOK_ROW, TOK_ROW, 0)
        adapter_output = apply_low_rank(normalized_input, adapter_row_picks, adapter_down_map, adapter_up_map)
        attn_sum = jnp.dot(attended, output_projection, preferred_element_type=jnp.float32) + adapter_output.astype(jnp.float32)
        return (token_rows.astype(jnp.float32) + attn_sum).astype(jnp.bfloat16)
    residual = lax.map(one_group, jnp.arange(N_ROW, dtype=jnp.int32)).reshape(TOKENS, MODEL_WIDTH)
    normed_mlp = rms_scaled(residual.astype(jnp.float32), feed_forward_gain).astype(jnp.bfloat16)
    gate = jnp.dot(normed_mlp, gate_projection, preferred_element_type=jnp.float32)
    up_part = jnp.dot(normed_mlp, up_projection, preferred_element_type=jnp.float32)
    hidden = (jax.nn.silu(gate) * up_part).astype(jnp.bfloat16)
    group_width = FF // N_COL
    accumulated = jnp.zeros((TOKENS, MODEL_WIDTH), jnp.float32)
    for group_idx in range(N_COL):
        lower = group_idx * group_width
        down_part = jnp.dot(hidden[:, lower:lower + group_width], down_projection[lower:lower + group_width], preferred_element_type=jnp.float32).astype(jnp.bfloat16)
        accumulated = accumulated + down_part.astype(jnp.float32)
    return (residual.astype(jnp.float32) + accumulated).astype(jnp.bfloat16)
```

```python
import functools

import jax
import jax.numpy as jnp
from jax import lax
from jax.experimental import pallas as pl
from jax.experimental.pallas import tpu as pltpu
from jax.sharding import PartitionSpec as P

HD = 112


epsilon = 1e-05


def rms_scaled(values, gain_row):
    mean_square = jnp.mean(values * values, axis=-1, keepdims=True)
    return values * lax.rsqrt(mean_square + epsilon) * gain_row


MESH = pl.DeviceIdType.MESH
NX, NY, NC = 4, 4, 2
ANY = pl.BlockSpec(memory_space=pl.ANY)
VMEM = pl.BlockSpec(memory_space=pltpu.VMEM)


def remote(source, target, send, recv, row, col):
    return pltpu.make_async_remote_copy(
        src_ref=source,
        dst_ref=target,
        send_sem=send,
        recv_sem=recv,
        device_id=(row, col),
        device_id_type=MESH,
    )


class Place:
    def __init__(self):
        self.row = lax.axis_index("row")
        self.z = lax.axis_index("col")
        self.count = lax.axis_size("col")
        self.row_count = lax.axis_size("row")
        self.c = lax.rem(self.row, NC)
        self.y = lax.rem(lax.div(self.row, NC), NY)
        self.x = lax.div(self.row, NC * NY)

    def col_at(self, offset):
        return lax.rem(self.z + offset + self.count, self.count)

    def x_at(self, offset):
        return lax.rem(self.x + offset + NX, NX)

    def y_at(self, offset):
        return lax.rem(self.y + offset + NY, NY)

    def row_of(self, x, y, c):
        return (x * NY + y) * NC + c

    def row_at(self, offset):
        return lax.rem(self.row + offset, self.row_count)

    def greet(self, reach):
        peers = [(self.row, self.col_at(1)), (self.row, self.col_at(-1))]
        if reach == "plane":
            for offset in range(1, NX):
                peers.append((self.row_of(self.x_at(offset), self.y, self.c), self.z))
            for offset in range(1, NY):
                peers.append((self.row_of(self.x, self.y_at(offset), self.c), self.z))
            peers.append((self.row_of(self.x, self.y, 1 - self.c), self.z))
        if reach == "row":
            for offset in range(1, self.row_count):
                peers.append((self.row_at(offset), self.z))
        barrier = pltpu.get_barrier_semaphore()
        for peer in peers:
            pl.semaphore_signal(barrier, inc=1, device_id=peer, device_id_type=MESH)
        return barrier, len(peers)


class RingGather:
    def __init__(self, place, own, whole, sends, recvs):
        self.place, self.own, self.whole = place, own, whole
        self.sends, self.recvs = sends, recvs
        self.hops = place.count // 2
        self.half = own.shape[0] // 2
        self.copies = {}

    def hop(self, k):
        place = self.place
        for u in range(2):
            for way in range(2):
                if k == self.hops - 1 and u != way:
                    continue
                if k > 0:
                    self.copies[k - 1, way, u].wait_recv()
                origin = place.col_at(-k if way == 0 else k)
                rows = pl.ds(u * self.half, self.half)
                source = self.own.at[rows] if k == 0 else self.whole.at[origin, rows]
                copy = remote(
                    source,
                    self.whole.at[origin, rows],
                    self.sends.at[k, way, u],
                    self.recvs.at[k, way, u],
                    place.row,
                    place.col_at(1 if way == 0 else -1),
                )
                copy.start()
                self.copies[k, way, u] = copy

    def finish(self):
        last = self.hops - 1
        for (k, way, u), copy in self.copies.items():
            copy.wait_send()
            if k == last or (k == last - 1 and u != way):
                copy.wait_recv()


class PlaneGather:
    def __init__(self, place, own, whole, cut, sends, recvs, local):
        self.place, self.own, self.whole = place, own, whole
        self.lanes = (pl.ds(0, cut), pl.ds(cut, own.shape[1] - cut))
        self.sends, self.recvs = sends, recvs
        self.local = pltpu.make_async_copy(own, whole.at[place.x, place.y, place.c], local)
        self.first, self.second, self.sibling = {}, {}, {}

    def group(self, path, offset):
        place, lanes = self.place, self.lanes[path]
        if path == 0:
            return self.whole.at[:, place.y_at(-offset), place.c, :, lanes]
        return self.whole.at[place.x_at(-offset), :, place.c, :, lanes]

    def peer(self, along_x, offset):
        place = self.place
        if along_x:
            return place.row_of(place.x_at(offset), place.y, place.c)
        return place.row_of(place.x, place.y_at(offset), place.c)

    def start(self):
        place = self.place
        self.local.start()
        for offset in range(1, 4):
            for path in range(2):
                lanes = self.lanes[path]
                copy = remote(
                    self.own.at[:, lanes],
                    self.whole.at[place.x, place.y, place.c, :, lanes],
                    self.sends.at[path, 0, offset],
                    self.recvs.at[path, 0, offset],
                    self.peer(path == 0, offset),
                    place.z,
                )
                copy.start()
                self.first[path, offset] = copy

    def hand_over(self, path, offset):
        place = self.place
        copy = remote(
            self.group(path, offset),
            self.group(path, offset),
            self.sends.at[path, 2, offset],
            self.recvs.at[path, 2, offset],
            place.row_of(place.x, place.y, 1 - place.c),
            place.z,
        )
        copy.start()
        self.sibling[path, offset] = copy

    def spread(self):
        self.local.wait()
        for path in range(2):
            for offset in range(1, 4):
                self.first[path, offset].wait_recv()
            for offset in range(1, 4):
                copy = remote(
                    self.group(path, 0),
                    self.group(path, 0),
                    self.sends.at[path, 1, offset],
                    self.recvs.at[path, 1, offset],
                    self.peer(path == 1, offset),
                    self.place.z,
                )
                copy.start()
                self.second[path, offset] = copy
            self.hand_over(path, 0)

    def share(self):
        for offset in range(1, 4):
            for path in range(2):
                self.second[path, offset].wait_recv()
                self.hand_over(path, offset)

    def finish(self):
        for copy in self.sibling.values():
            copy.wait_recv()
        for group in (self.first, self.second, self.sibling):
            for copy in group.values():
                copy.wait_send()


class RingSum:
    def __init__(self, place, part, stage, land_half, land, sends, recvs):
        self.place, self.part, self.stage = place, part, stage
        self.land_half, self.land, self.sends, self.recvs = land_half, land, sends, recvs
        self.hops = place.count // 2
        self.half = part.shape[1] // 2
        self.cols = part.shape[2] // 2
        self.copies = {}

    def hop(self, k):
        place, half = self.place, self.half
        for h in range(2):
            cols = pl.ds(h * self.cols, self.cols)
            for way in range(2):
                left = self.hops - k
                block = place.col_at(left if way == 0 else -left)
                if k == 0:
                    source = self.part.at[block, pl.ds(way * half, half), cols]
                    target = self.land_half.at[way, h]
                else:
                    self.copies[k - 1, way, h].wait_recv()
                    stage = self.stage.at[k - 1, way, h]
                    if k == 1:
                        got = pl.ds(way * half, half)
                        rest = pl.ds((1 - way) * half, half)
                        stage[got] = (
                            self.part[block, got, cols].astype(jnp.float32)
                            + self.land_half[way, h].astype(jnp.float32)
                        ).astype(jnp.bfloat16)
                        stage[rest] = self.part[block, rest, cols]
                    else:
                        stage[...] = (
                            self.part[block, :, cols].astype(jnp.float32)
                            + self.land[k - 2, way, h].astype(jnp.float32)
                        ).astype(jnp.bfloat16)
                    source = stage
                    target = self.land.at[k - 1, way, h]
                copy = remote(
                    source,
                    target,
                    self.sends.at[k, way, h],
                    self.recvs.at[k, way, h],
                    place.row,
                    place.col_at(1 if way == 0 else -1),
                )
                copy.start()
                self.copies[k, way, h] = copy

    def total(self, h):
        last = self.hops - 1
        for way in range(2):
            self.copies[last, way, h].wait_recv()
        cols = pl.ds(h * self.cols, self.cols)
        return (
            self.part[self.place.z, :, cols].astype(jnp.float32)
            + self.land[last - 1, 0, h].astype(jnp.float32)
            + self.land[last - 1, 1, h].astype(jnp.float32)
        )

    def finish(self):
        for copy in self.copies.values():
            copy.wait_send()


def ring_sum_scratch(count, block_rows, width):
    hops = count // 2
    return [
        pltpu.VMEM((hops - 1, 2, 2, block_rows, width // 2), jnp.bfloat16),
        pltpu.VMEM((2, 2, block_rows // 2, width // 2), jnp.bfloat16),
        pltpu.VMEM((hops - 1, 2, 2, block_rows, width // 2), jnp.bfloat16),
    ] + ring_semaphores(count)


def ring_semaphores(count):
    return [pltpu.SemaphoreType.DMA((count // 2, 2, 2)), pltpu.SemaphoreType.DMA((count // 2, 2, 2))]


def plane_semaphores():
    return [
        pltpu.SemaphoreType.DMA((2, 3, 4)),
        pltpu.SemaphoreType.DMA((2, 3, 4)),
        pltpu.SemaphoreType.DMA,
    ]


class Exchange:
    def __init__(self, place, outgoing, incoming, send, recv):
        self.place, self.outgoing, self.incoming = place, outgoing, incoming
        self.send, self.recv = send, recv

    def start(self):
        place = self.place
        for offset in range(1, place.row_count):
            peer = place.row_at(offset)
            remote(
                self.outgoing.at[peer],
                self.incoming.at[place.row],
                self.send,
                self.recv,
                peer,
                place.z,
            ).start()
        self.incoming[place.row] = self.outgoing[place.row]

    def all_but_one(self, ref, semaphore):
        blocks = ref.at[pl.ds(0, self.place.row_count - 1)]
        return pltpu.make_async_copy(blocks, blocks, semaphore)

    def arrived(self):
        self.all_but_one(self.incoming, self.recv).wait()

    def finish(self):
        self.all_but_one(self.outgoing, self.send).wait()


def placer_of(ids_col, capacity, slots):
    count = ids_col.shape[0]
    down = lax.broadcasted_iota(jnp.int32, (count, count), 0)
    across = lax.broadcasted_iota(jnp.int32, (count, count), 1)
    ids_row = jnp.sum(jnp.where(down == across, ids_col, 0), axis=0, keepdims=True)
    same_before = (ids_col == ids_row) & (down < across)
    rank = jnp.sum(same_before.astype(jnp.int32), axis=0, keepdims=True)
    target = ids_row * capacity + rank
    slot = lax.broadcasted_iota(jnp.int32, (slots, count), 0)
    return jnp.where(slot == target, 1.0, 0.0).astype(jnp.bfloat16)


def open_body(
    cut, capacity, own, own_hbm, gain, ids, down_map, up_map, weights, tokens, base, weight_rows, *scratch
):
    place = Place()
    ring = RingGather(place, own_hbm, tokens, scratch[0], scratch[1])
    plane = PlaneGather(place, weights, weight_rows, cut, scratch[2], scratch[3], scratch[4])
    kept = pltpu.make_async_copy(own_hbm, tokens.at[place.z], scratch[5])
    asked, asking, answer, answered = scratch[6:10]
    there = Exchange(place, asked, asking, scratch[10], scratch[11])
    back = Exchange(place, answer, answered, scratch[12], scratch[13])
    own_count, width = own.shape
    rows, per_row, _ = asked.shape
    slots = rows * per_row

    met = place.greet("row")
    own_rows = rms_scaled(own[...].astype(jnp.float32), gain[...]).astype(jnp.bfloat16)
    first_row = pl.multiple_of(place.z * own_count, own_count)
    placer = placer_of(ids[pl.ds(first_row, own_count), :], capacity, slots)
    outgoing = jnp.dot(placer, own_rows, preferred_element_type=jnp.float32)
    asked[...] = outgoing.reshape(rows, per_row, width).astype(jnp.bfloat16)
    pl.semaphore_wait(*met)
    ring.hop(0)
    plane.start()
    there.start()
    kept.start()
    plane.spread()
    ring.hop(1)

    there.arrived()
    received = asking[...].reshape(slots, width)
    slot = lax.broadcasted_iota(jnp.int32, (slots, 1), 0)
    adapter = lax.rem(lax.div(slot, capacity), down_map.shape[0])
    result = jnp.zeros((slots, width), jnp.float32)
    for kept_one in range(down_map.shape[0]):
        low = jnp.dot(received, down_map[kept_one], preferred_element_type=jnp.float32)
        low = jnp.where(adapter == kept_one, low, 0.0).astype(jnp.bfloat16)
        result = result + jnp.dot(low, up_map[kept_one], preferred_element_type=jnp.float32)
    answer[...] = result.reshape(rows, per_row, width).astype(jnp.bfloat16)
    back.start()

    ring.hop(2)
    plane.share()
    ring.hop(3)
    back.arrived()
    base[...] = own[...].astype(jnp.float32) + lax.dot_general(
        placer,
        answered[...].reshape(slots, width),
        (((0,), (0,)), ((), ())),
        preferred_element_type=jnp.float32,
    )
    kept.wait()
    there.finish()
    back.finish()
    ring.finish()
    plane.finish()


def attend_body(
    lengths, valid, tokens, gain, weights, taps, cache, out, normed, mixed, attended
):
    tok_count = tokens.shape[0]
    heads_wide = attended.shape[1]
    requests, _, head_count, window, head = cache.shape
    for lower in range(0, tok_count, 128):
        rows = pl.ds(lower, 128)
        normed[rows] = rms_scaled(tokens[rows].astype(jnp.float32), gain[...]).astype(jnp.bfloat16)
    mixed[...] = jnp.dot(normed[...], weights[...], preferred_element_type=jnp.float32)

    spot = lax.broadcasted_iota(jnp.int32, (tok_count, 1), 0)
    segment = jnp.zeros((tok_count, 1), jnp.int32)
    begin = jnp.zeros((tok_count, 1), jnp.int32)
    finish = 0
    for request in range(requests):
        finish = finish + lengths[0, request]
        past = spot >= finish
        segment = segment + past.astype(jnp.int32)
        begin = jnp.where(past, finish, begin)
    held = jnp.zeros((tok_count, 1), jnp.int32)
    for request in range(requests):
        held = jnp.where(segment == request, valid[0, request], held)
    inside = spot - begin
    first_key = jnp.maximum(begin, spot - (window - 1))
    first_slot = segment * window + jnp.maximum(window - held, inside + 1)
    last_slot = segment * window + (window - 1)

    def convolved(values, which):
        total = taps[0, which : which + 1, :] * values
        for offset in range(1, taps.shape[0]):
            moved = jnp.where(inside >= offset, pltpu.roll(values, offset, 0), 0.0)
            total = total + taps[offset, which : which + 1, :] * moved
        return total

    queries = mixed[:, heads_wide : 2 * heads_wide].astype(jnp.bfloat16)
    keys_used = convolved(mixed[:, 2 * heads_wide : 3 * heads_wide], 0).astype(jnp.bfloat16)
    raw_values = mixed[:, 3 * heads_wide :]
    values_used = (raw_values * jax.nn.sigmoid(convolved(raw_values, 1))).astype(jnp.bfloat16)

    scale = head ** (-0.5)
    step = 128
    both = (((1,), (1,)), ((), ()))
    for lower in range(0, tok_count, step):
        upper = lower + step
        start = max(0, lower - window)
        key_spot = start + lax.broadcasted_iota(jnp.int32, (step, upper - start), 1)
        near = (key_spot <= spot[lower:upper]) & (key_spot >= first_key[lower:upper])
        slot = lax.broadcasted_iota(jnp.int32, (step, requests * window), 1)
        cached = (slot >= first_slot[lower:upper]) & (slot <= last_slot[lower:upper])
        pieces = []
        for h in range(head_count):
            cols = slice(h * head, (h + 1) * head)
            query = queries[lower:upper, cols]
            near_scores = scale * lax.dot_general(
                query, keys_used[start:upper, cols], both, preferred_element_type=jnp.float32
            )
            cached_scores = scale * lax.dot_general(
                query,
                cache[:, 0, h].reshape(requests * window, head),
                both,
                preferred_element_type=jnp.float32,
            )
            near_scores = jnp.where(near, near_scores, -jnp.inf)
            cached_scores = jnp.where(cached, cached_scores, -jnp.inf)
            most = jnp.maximum(
                jnp.max(near_scores, axis=-1, keepdims=True),
                jnp.max(cached_scores, axis=-1, keepdims=True),
            )
            near_exp = jnp.exp(near_scores - most)
            cached_exp = jnp.exp(cached_scores - most)
            total = jnp.sum(near_exp, axis=-1, keepdims=True) + jnp.sum(
                cached_exp, axis=-1, keepdims=True
            )
            inverse = 1.0 / total
            pieces.append(
                jnp.dot(
                    (near_exp * inverse).astype(jnp.bfloat16),
                    values_used[start:upper, cols],
                    preferred_element_type=jnp.float32,
                )
                + jnp.dot(
                    (cached_exp * inverse).astype(jnp.bfloat16),
                    cache[:, 1, h].reshape(requests * window, head),
                    preferred_element_type=jnp.float32,
                )
            )
        attended[lower:upper, :] = jnp.concatenate(pieces, axis=1).astype(jnp.bfloat16)
    out[...] = lax.dot_general(
        attended[...], weights[:, :heads_wide], both, preferred_element_type=jnp.float32
    ).astype(jnp.bfloat16)


def feed_body(tokens, gain, weights, out, normed):
    tok_count = tokens.shape[0]
    hidden_count = weights.shape[1] // 3
    for lower in range(0, tok_count, 128):
        rows = pl.ds(lower, 128)
        normed[rows] = rms_scaled(tokens[rows].astype(jnp.float32), gain[...]).astype(jnp.bfloat16)
    gate = jnp.dot(normed[...], weights[:, :hidden_count], preferred_element_type=jnp.float32)
    up_part = jnp.dot(
        normed[...], weights[:, hidden_count : 2 * hidden_count], preferred_element_type=jnp.float32
    )
    hidden = (jax.nn.silu(gate) * up_part).astype(jnp.bfloat16)
    out[...] = lax.dot_general(
        hidden,
        weights[:, 2 * hidden_count :],
        (((1,), (1,)), ((), ())),
        preferred_element_type=jnp.float32,
    ).astype(jnp.bfloat16)


def middle_body(cut, part, base, weights, tokens, residual, weight_rows, *scratch):
    place = Place()
    sums = RingSum(place, part, *scratch[0:5])
    ring = RingGather(place, residual, tokens, scratch[5], scratch[6])
    plane = PlaneGather(place, weights, weight_rows, cut, scratch[7], scratch[8], scratch[9])
    kept = pltpu.make_async_copy(residual, tokens.at[place.z], scratch[10])
    pl.semaphore_wait(*place.greet("plane"))
    sums.hop(0)
    plane.start()
    sums.hop(1)
    plane.spread()
    sums.hop(2)
    sums.hop(3)
    for h in range(2):
        cols = pl.ds(h * sums.cols, sums.cols)
        residual[:, cols] = (base[:, cols] + sums.total(h)).astype(jnp.bfloat16)
    ring.hop(0)
    kept.start()
    plane.share()
    ring.hop(1)
    ring.hop(2)
    ring.hop(3)
    kept.wait()
    sums.finish()
    ring.finish()
    plane.finish()


def close_body(part, base, out, *scratch):
    place = Place()
    sums = RingSum(place, part, *scratch)
    pl.semaphore_wait(*place.greet("ring"))
    for k in range(sums.hops):
        sums.hop(k)
    for h in range(2):
        cols = pl.ds(h * sums.cols, sums.cols)
        out[:, cols] = (base[:, cols].astype(jnp.float32) + sums.total(h)).astype(jnp.bfloat16)
    sums.finish()


def params(number):
    return pltpu.CompilerParams(
        collective_id=number, has_side_effects=True, vmem_limit_bytes=40 * 1024 * 1024
    )


def open_exchange(own, gain, ids, down_map, up_map, weights, count, rows):
    block_rows, width = own.shape
    weight_rows, lanes = weights.shape
    kept_count = down_map.shape[0]
    capacity = max(2, 2 * block_rows // (kept_count * rows))
    slots = pltpu.VMEM((rows, kept_count * capacity, width), jnp.bfloat16)
    return pl.pallas_call(
        functools.partial(open_body, lanes // 256 * 128, capacity),
        out_shape=(
            jax.ShapeDtypeStruct((count, block_rows, width), jnp.bfloat16),
            jax.ShapeDtypeStruct((block_rows, width), jnp.float32),
            jax.ShapeDtypeStruct((NX, NY, NC, weight_rows, lanes), jnp.bfloat16),
        ),
        in_specs=[VMEM, ANY, VMEM, VMEM, VMEM, VMEM, ANY],
        out_specs=(ANY, VMEM, ANY),
        scratch_shapes=ring_semaphores(count)
        + plane_semaphores()
        + [pltpu.SemaphoreType.DMA, slots, slots, slots, slots]
        + [pltpu.SemaphoreType.DMA] * 4,
        compiler_params=params(0),
        cost_estimate=pl.CostEstimate(flops=0, bytes_accessed=60_000_000, transcendentals=0),
        name="gather_tokens_and_weights",
    )(own, own, gain, ids, down_map, up_map, weights)


def attention(lengths, valid, tokens, gain, weights, taps, cache):
    tok_count, width = tokens.shape
    lanes = weights.shape[1]
    scalars = pl.BlockSpec(memory_space=pltpu.SMEM)
    return pl.pallas_call(
        attend_body,
        out_shape=jax.ShapeDtypeStruct((tok_count, width), jnp.bfloat16),
        in_specs=[scalars, scalars] + [VMEM] * 5,
        out_specs=VMEM,
        scratch_shapes=[
            pltpu.VMEM((tok_count, width), jnp.bfloat16),
            pltpu.VMEM((tok_count, lanes), jnp.float32),
            pltpu.VMEM((tok_count, lanes // 4), jnp.bfloat16),
        ],
        compiler_params=pltpu.CompilerParams(vmem_limit_bytes=48 * 1024 * 1024),
        name="attention",
    )(lengths, valid, tokens, gain, weights, taps, cache)


def feed_forward(tokens, gain, weights):
    tok_count, width = tokens.shape
    return pl.pallas_call(
        feed_body,
        out_shape=jax.ShapeDtypeStruct((tok_count, width), jnp.bfloat16),
        in_specs=[VMEM] * 3,
        out_specs=VMEM,
        scratch_shapes=[pltpu.VMEM((tok_count, width), jnp.bfloat16)],
        compiler_params=pltpu.CompilerParams(vmem_limit_bytes=48 * 1024 * 1024),
        name="feed_forward",
    )(tokens, gain, weights)


def middle_exchange(part, base, weights):
    count, block_rows, width = part.shape
    weight_rows, lanes = weights.shape
    return pl.pallas_call(
        functools.partial(middle_body, lanes // 256 * 128),
        out_shape=(
            jax.ShapeDtypeStruct((count, block_rows, width), jnp.bfloat16),
            jax.ShapeDtypeStruct((block_rows, width), jnp.bfloat16),
            jax.ShapeDtypeStruct((NX, NY, NC, weight_rows, lanes), jnp.bfloat16),
        ),
        in_specs=[VMEM, VMEM, ANY],
        out_specs=(ANY, VMEM, ANY),
        scratch_shapes=ring_sum_scratch(count, block_rows, width)
        + ring_semaphores(count)
        + plane_semaphores()
        + [pltpu.SemaphoreType.DMA],
        compiler_params=params(1),
        cost_estimate=pl.CostEstimate(flops=0, bytes_accessed=100_000_000, transcendentals=0),
        name="sum_then_gather",
    )(part, base, weights)


def close_exchange(part, base):
    count, block_rows, width = part.shape
    return pl.pallas_call(
        close_body,
        out_shape=jax.ShapeDtypeStruct((block_rows, width), jnp.bfloat16),
        in_specs=[VMEM, VMEM],
        out_specs=VMEM,
        scratch_shapes=ring_sum_scratch(count, block_rows, width),
        compiler_params=params(2),
        cost_estimate=pl.CostEstimate(flops=0, bytes_accessed=50_000_000, transcendentals=0),
        name="sum_hidden_units",
    )(part, base)


def on_device(
    inputs,
    attention_norm_gain,
    query_key_value_weight,
    filter_taps,
    output_projection,
    window_key_value,
    cache_valid_length,
    lengths,
    token_adapter_index,
    adapter_down_map,
    adapter_up_map,
    feed_forward_gain,
    gate_projection,
    up_projection,
    down_projection,
):
    own_count, width = inputs.shape
    row_count = lax.axis_size("row")
    col_count = lax.axis_size("col")
    tok_count = col_count * own_count
    head_cols = filter_taps.shape[2]
    qkv_rows = query_key_value_weight.shape[0]

    first_weights = jnp.concatenate(
        [
            jnp.transpose(output_projection),
            query_key_value_weight.reshape(qkv_rows, 3 * head_cols),
        ],
        axis=1,
    )
    later_weights = jnp.concatenate(
        [gate_projection, up_projection, jnp.transpose(down_projection)], axis=1
    )
    gathered, base, first_rows = open_exchange(
        inputs,
        attention_norm_gain[None, :],
        token_adapter_index,
        adapter_down_map,
        adapter_up_map,
        first_weights,
        col_count,
        row_count,
    )
    requests, _, heads, merged = window_key_value.shape
    out_term = attention(
        lengths,
        cache_valid_length[None, :],
        gathered.reshape(tok_count, width),
        attention_norm_gain[None, :],
        first_rows.reshape(width, 4 * head_cols),
        filter_taps,
        window_key_value.reshape(requests, 2, heads, merged // HD, HD),
    )
    whole_mixed, residual, later_rows = middle_exchange(
        out_term.reshape(col_count, own_count, width), base, later_weights
    )
    down_term = feed_forward(
        whole_mixed.reshape(tok_count, width),
        feed_forward_gain[None, :],
        later_rows.reshape(width, 3 * gate_projection.shape[1]),
    )
    return close_exchange(down_term.reshape(col_count, own_count, width), residual)


def solution(mesh):
    placed = (
        P(("row", "col"), None),
        P(),
        P("row", None, "col"),
        P(None, None, "col"),
        P("col", "row"),
        P("row", None, "col", None),
        P("row"),
        P("row", None),
        P("row", None),
        P("row", None, None),
        P("row", None, None),
        P(),
        P("row", "col"),
        P("row", "col"),
        P("col", "row"),
    )
    return jax.shard_map(
        on_device, mesh=mesh, in_specs=placed, out_specs=P(("row", "col"), None), check_vma=False
    )
```
